32 devices in a mesh: groups: 2 (over x), seq: 4 (over y, core), sub: 4 (over z).
Axes of the slice: x: 2, y: 2, z: 4, core: 2. Of those that a mesh axis runs over, the one named last changes fastest.
Arguments:
- queries: bfloat16 [65536, 512], P(('groups', 'seq', 'sub')), parts along dimension 0, may hold values from -6 to 6
- key_rows: bfloat16 [65536, 512], P(('groups', 'seq', 'sub')), parts along dimension 0, may hold values from -6 to 6
- value_rows: bfloat16 [65536, 512], P(('groups', 'seq', 'sub')), parts along dimension 0, may hold values from -6 to 6
- level_index: int32 [65536], P(('groups', 'seq', 'sub')), parts along dimension 0, may hold values from 0 to 15
- level_table: float32 [16, 20, 4], replicated, may hold values from 0.0001 to 4.5, as said below
- out_gain: float32 [512], replicated, may hold values from 0.5 to 1.5
Outputs:
- mixed: bfloat16 [65536, 512], P(('groups', 'seq', 'sub')), parts along dimension 0
The draws below stay inside these ranges and needn't reach their ends.
There are 2 independent parts, one for each index of `groups`. The reference program is written for one: setup_inputs(seed, part) draws one part's arguments, and reference() takes and returns one part's arrays. A program takes and returns all parts, laid end to end along the dimension named above; an argument that names none is the same for every part. Nothing has to cross between parts.
Inputs may be any that keep to these rules, and one draw needn't show every extreme that they name: `level_table`: every weight of the table is positive.
All inputs are finite; a program needn't handle non-finite values.
Results may differ from the reference program's by a relative error of at most 0.0048.
Values sent between devices are 32-bit elements; how exact they have to be, the bound alone decides.
No kernel may reach another device: no remote copies, remote signals or barrier semaphores. Data moves between devices by JAX's collectives and lax.ppermute only.
A program may use at most 128 MiB of HBM per device.

```python
import jax
import jax.numpy as jnp
from jax import lax

HEADS = 4
HD = 128
LEVELS = 20
NTAB = 16
TOK_DEV = 2048
TOKENS = 32768


def draw_level_table(key, part):
    level_pos = jnp.arange(LEVELS, dtype=jnp.int32)
    spanned = (jnp.maximum(level_pos, 1) - 1).astype(jnp.float32)
    level_scale = jnp.exp2(-0.5 * spanned)
    spread = jax.random.uniform(key, (NTAB, LEVELS, HEADS), jnp.float32, -1.5, 1.5)
    return jnp.exp(spread) * level_scale[None, :, None]


def set_ends(drawn, own_key, least, high):
    shape = drawn.shape
    spot = [jax.random.randint(jax.random.fold_in(own_key, axis), (), 0, shape[axis]) for axis in range(len(shape))]
    drawn = drawn.at[tuple(spot)].set(least)
    longest = shape.index(max(shape))
    spot[longest] = (spot[longest] + 1) % shape[longest]
    return drawn.at[tuple(spot)].set(high)


def block_scale(stream_key, dims, shards, least, top_value):
    factor_of = 1.0
    for dim, blocks in shards:
        heights = jax.random.uniform(jax.random.fold_in(jax.random.fold_in(stream_key, 6), dim), (blocks,), jnp.float32, least / len(shards), top_value / len(shards))
        factor_of = factor_of * jnp.repeat(jnp.exp(heights), dims[dim] // blocks).reshape((-1,) + (1,) * (len(dims) - 1 - dim))
    return factor_of


def noise(rng, shape, width, reach, cuts=(), kind=jnp.bfloat16):
    gain = block_scale(rng, shape, cuts, -0.22, 0.18) if cuts else 1.0
    values = jax.random.normal(rng, shape, jnp.float32) * width * gain
    return jnp.minimum(jnp.maximum(values, -reach), reach).astype(kind)


def setup_inputs(seed: int = 0, part: int = 0) -> dict:
    key_list = jax.random.split(jax.random.key(seed), 7)
    part_splits = jax.random.split(jax.random.fold_in(key_list[6], part), 7)
    queries = noise(part_splits[0], (TOKENS, HEADS * HD), 1.0, 6.0, ((0, 16),))
    key_rows = noise(part_splits[1], (TOKENS, HEADS * HD), 1.0, 6.0, ((0, 16),))
    value_rows = noise(part_splits[2], (TOKENS, HEADS * HD), 1.0, 6.0, ((0, 16),))
    level_index = set_ends(jax.random.randint(part_splits[3], (TOKENS,), 0, NTAB), jax.random.fold_in(part_splits[3], 1), 0, NTAB - 1).astype(jnp.int32)
    level_table = draw_level_table(jax.random.fold_in(key_list[6], 71), part)
    out_gain = jnp.clip(1.0 + 0.1 * jax.random.normal(key_list[5], (HEADS * HD,), jnp.float32), 0.5, 1.5)
    return {"queries": queries, "key_rows": key_rows, "value_rows": value_rows, "level_index": level_index, "level_table": level_table, "out_gain": out_gain}


eps_norm = 1e-06
row_limit = 512

def level_of(rows_pos, cols_pos, span_rows):
    mixed_bits = jnp.bitwise_xor(rows_pos, cols_pos)
    level_count = jnp.zeros(mixed_bits.shape, jnp.int32)
    for bit_pos in range(span_rows.bit_length()):
        level_count = level_count + (mixed_bits >= 1 << bit_pos).astype(jnp.int32)
    return level_count

def near_terms(queries, key_rows, value_rows, weights):
    tok_count = queries.shape[0]
    block_rows = min(row_limit, tok_count)
    pieces = []
    for start_row in range(0, tok_count, block_rows):
        stop_row = start_row + block_rows
        rows_pos = jnp.arange(start_row, stop_row, dtype=jnp.int32)
        cols_pos = jnp.arange(0, stop_row, dtype=jnp.int32)
        levels = level_of(rows_pos[:, None], cols_pos[None, :], tok_count)
        causal = cols_pos[None, :] <= rows_pos[:, None]
        head_parts = []
        for head_id in range(HEADS):
            first_col = head_id * HD
            q_block = queries[start_row:stop_row, first_col:first_col + HD]
            k_block = key_rows[:stop_row, first_col:first_col + HD]
            v_block = value_rows[:stop_row, first_col:first_col + HD]
            scores = jnp.dot(q_block, k_block.T, preferred_element_type=jnp.float32)
            picked = jnp.take_along_axis(weights[start_row:stop_row, :, head_id], levels, axis=1)
            weighted = jnp.where(causal, picked * scores, 0.0).astype(jnp.bfloat16)
            head_parts.append(jnp.dot(weighted, v_block, preferred_element_type=jnp.float32))
        pieces.append(jnp.concatenate(head_parts, axis=1))
    return jnp.concatenate(pieces, axis=0)

def normalize_heads(attended, out_gain):
    per_head = attended.reshape(attended.shape[0], HEADS, HD)
    mean_sq = lax.optimization_barrier(jnp.mean(per_head * per_head, axis=-1, keepdims=True))
    normed = per_head * lax.rsqrt(mean_sq + eps_norm)
    return (normed.reshape(attended.shape[0], HEADS * HD) * out_gain).astype(jnp.bfloat16)

def reference(queries, key_rows, value_rows, level_index, level_table, out_gain):
    tok_count = TOK_DEV
    n_stretches = queries.shape[0] // tok_count
    stretch_bits = tok_count.bit_length() - 1
    tree_bits = n_stretches.bit_length() - 1
    weights_all = level_table[level_index]

    def stretch_view(array):
        return array.reshape((n_stretches, tok_count) + array.shape[1:])

    def one_state(inputs):
        k_stretch, v_stretch = inputs
        k_three = k_stretch.astype(jnp.float32).reshape(tok_count, HEADS, HD)
        v_three = v_stretch.astype(jnp.float32).reshape(tok_count, HEADS, HD)
        return jnp.einsum('thd,the->hde', k_three, v_three, precision=lax.Precision.HIGHEST)
    stretch_states = lax.map(one_state, (stretch_view(key_rows), stretch_view(value_rows)))
    tree = [stretch_states]
    for level_bit in range(1, tree_bits):
        previous = tree[-1]
        tree.append(previous.reshape((previous.shape[0] // 2, 2) + previous.shape[1:]).sum(1))

    def one_stretch(inputs):
        stretch_id, q_stretch, k_stretch, v_stretch, w_stretch = inputs
        near = near_terms(q_stretch, k_stretch, v_stretch, w_stretch)
        q_three = q_stretch.astype(jnp.float32).reshape(tok_count, HEADS, HD)
        far = jnp.zeros((tok_count, HEADS, HD), jnp.float32)
        for level_bit in range(tree_bits):
            owner = jnp.right_shift(stretch_id, level_bit)
            present = (owner % 2).astype(jnp.float32)
            sibling = jnp.bitwise_xor(owner, 1).astype(jnp.int32)
            state = lax.dynamic_index_in_dim(tree[level_bit], sibling, 0, keepdims=False)
            rounded = lax.optimization_barrier((state * present).astype(jnp.bfloat16))
            term = jnp.einsum('thd,hde->the', q_three, rounded.astype(jnp.float32), precision=lax.Precision.HIGHEST)
            far = far + w_stretch[:, stretch_bits + 1 + level_bit, :, None] * term
        attended = near + far.reshape(tok_count, HEADS * HD)
        return normalize_heads(attended, out_gain)
    stretch_ids = jnp.arange(n_stretches, dtype=jnp.int32)
    mixed = lax.map(one_stretch, (stretch_ids, stretch_view(queries), stretch_view(key_rows), stretch_view(value_rows), stretch_view(weights_all)))
    return mixed.reshape(queries.shape[0], HEADS * HD)
```

```python
import functools

import jax
import jax.numpy as jnp
from jax import lax
from jax.experimental import pallas as pl
from jax.experimental.pallas import tpu as pltpu
from jax.sharding import PartitionSpec as P

EPS = 1e-06
LANES = 128
LEAF = 256
F32 = jnp.float32
BF16 = jnp.bfloat16


def bits_of(size):
    return size.bit_length() - 1


def swapped(block, axis, apart):
    count = lax.axis_size(axis)
    route = []
    for low in range(count):
        high = low | 1 << apart
        if high != low and high < count:
            route += [(low, high), (high, low)]
    return lax.ppermute(block, axis, route)


def whole(shape):
    return pl.BlockSpec(shape, lambda *_: (0,) * len(shape))


def rows(block):
    return pl.BlockSpec(block, lambda i: (i,) + (0,) * (len(block) - 1))


def state_kernel(heads, k_ref, v_ref, total_ref, part_ref, acc_ref):
    step = pl.program_id(0)
    n_leaf = pl.num_programs(0)
    hd = k_ref.shape[1] // heads
    depth = acc_ref.shape[0]
    for h in range(heads):
        cols = slice(h * hd, (h + 1) * hd)
        value = lax.dot_general(
            k_ref[:, cols], v_ref[:, cols], (((0,), (0,)), ((), ())), preferred_element_type=F32
        )
        acc_ref[0, h] = value
    base = 0
    count = part_ref.shape[0] + 1
    for level in range(depth):
        count = count // 2
        done = (step + 1) % (1 << level) == 0
        lower = (step >> level) % 2 == 0

        @pl.when(done & lower)
        def _(level=level, base=base):
            part_ref[base + (step >> (level + 1))] = acc_ref[level].astype(BF16)
            if level + 1 < depth:
                acc_ref[level + 1] = acc_ref[level]

        @pl.when(done & jnp.logical_not(lower))
        def _(level=level):
            if level + 1 < depth:
                acc_ref[level + 1] = acc_ref[level + 1] + acc_ref[level]
            else:
                total_ref[...] = total_ref[...] + acc_ref[level]

        if level + 1 == depth:

            @pl.when(done & lower)
            def _(level=level):
                total_ref[...] = acc_ref[level]

        base += count


def level_lanes(size, heads):
    t = lax.broadcasted_iota(jnp.int32, (size, size), 0)
    s = lax.broadcasted_iota(jnp.int32, (size, size), 1)
    mixed = jnp.bitwise_xor(t, s)
    level = jnp.zeros_like(mixed)
    for bit in range(bits_of(size)):
        level = level + (mixed >= (1 << bit)).astype(jnp.int32)
    return jnp.where(s <= t, level * heads, LANES - heads)


def near_kernel(heads, leaf_level, idx_ref, tbl_ref, q_ref, k_ref, v_ref, st_ref, out_ref, w_ref, lane_ref):
    step = pl.program_id(0)
    hd = q_ref.shape[1] // heads
    n_state = st_ref.shape[0]
    sub_rows = LANES
    parts = q_ref.shape[0] // sub_rows

    @pl.when(step == 0)
    def _():
        lane_ref[...] = level_lanes(sub_rows, heads)

    ntab = tbl_ref.shape[0]
    table = tbl_ref[...]
    hi = table.astype(BF16)
    rest = table - hi.astype(F32)
    mid = rest.astype(BF16)
    low = (rest - mid.astype(F32)).astype(BF16)
    pieces = jnp.concatenate([hi, mid, low], axis=0)
    ws = []
    for part in range(parts):
        index = idx_ref[pl.ds(step * parts + part, 1), :]
        hit = lax.broadcasted_iota(jnp.int32, (ntab, sub_rows), 0) == index
        hot = jnp.where(hit, 1.0, 0.0).astype(BF16)
        hot = jnp.concatenate([hot, hot, hot], axis=0)
        w = lax.dot_general(hot, pieces, (((0,), (0,)), ((), ())), preferred_element_type=F32)
        w_ref[part * sub_rows : (part + 1) * sub_rows, :] = w
        ws.append(w)
    lanes = lane_ref[...]
    for h in range(heads):
        cols = slice(h * hd, (h + 1) * hd)
        k = k_ref[:, cols]
        v = v_ref[:, cols]
        for part in range(parts):
            top = (part + 1) * sub_rows
            here = slice(part * sub_rows, top)
            q = q_ref[here, cols]
            scores = lax.dot_general(q, k[:top], (((1,), (1,)), ((), ())), preferred_element_type=F32)
            picked = []
            for other in range(part):
                gap = bits_of(sub_rows) + (part ^ other).bit_length()
                lane = gap * heads + h
                block = scores[:, other * sub_rows : (other + 1) * sub_rows]
                picked.append((ws[part][:, lane : lane + 1] * block).astype(BF16))
            diag = jnp.take_along_axis(ws[part], lanes + h, axis=1)
            picked.append((diag * scores[:, part * sub_rows :]).astype(BF16))
            weighted = picked[0] if len(picked) == 1 else jnp.concatenate(picked, axis=1)
            out_ref[here, cols] = jnp.dot(weighted, v[:top], preferred_element_type=F32)
    base = 0
    count = n_state + 1
    for level in range(bits_of(n_state + 1)):
        count = count // 2

        @pl.when((step >> level) % 2 == 1)
        def _(level=level, base=base):
            for h in range(heads):
                cols = slice(h * hd, (h + 1) * hd)
                lane = (leaf_level + 1 + level) * heads + h
                term = jnp.dot(q_ref[:, cols], st_ref[base + (step >> (level + 1)), h], preferred_element_type=F32)
                out_ref[:, cols] = out_ref[:, cols] + w_ref[:, lane : lane + 1] * term

        base += count


def far_kernel(heads, first_level, axis, last, *refs):
    if last:
        gain_ref, att_ref, q_ref, w_ref, *state_refs, out_ref, stack_ref = refs
    else:
        att_ref, q_ref, w_ref, *state_refs, out_ref, stack_ref = refs
    hd = q_ref.shape[1] // heads
    n = len(state_refs)

    @pl.when(pl.program_id(0) == 0)
    def _():
        place = lax.axis_index(axis)
        for j, state_ref in enumerate(state_refs):
            upper = ((place >> j) % 2).astype(F32)
            for h in range(heads):
                stack_ref[h, :, j * hd : (j + 1) * hd] = (state_ref[h] * upper).astype(BF16)

    w = w_ref[...]
    for h in range(heads):
        cols = slice(h * hd, (h + 1) * hd)
        term = jnp.dot(q_ref[:, cols], stack_ref[h], preferred_element_type=F32)
        total = att_ref[:, cols]
        for j in range(n):
            lane = (first_level + j) * heads + h
            total = total + w[:, lane : lane + 1] * term[:, j * hd : (j + 1) * hd]
        if last:
            mean = jnp.mean(total * total, axis=-1, keepdims=True)
            total = total * lax.rsqrt(mean + EPS) * gain_ref[:, cols]
        out_ref[:, cols] = total.astype(out_ref.dtype)


def on_device(queries, key_rows, value_rows, level_index, level_table, out_gain):
    tok, width = queries.shape
    ntab, levels, heads = level_table.shape
    hd = width // heads
    leaf = min(LEAF, tok)
    n_leaf = tok // leaf
    depth = bits_of(n_leaf)
    token_bits = bits_of(tok)
    grid = (n_leaf,)
    table = jnp.pad(level_table.reshape(ntab, levels * heads), ((0, 0), (0, LANES - levels * heads)))
    index = level_index.reshape(tok // LANES, LANES)
    gain = out_gain.reshape(1, width)
    state_shape = (heads, hd, hd)
    sds = jax.ShapeDtypeStruct
    total, parts = pl.pallas_call(
        functools.partial(state_kernel, heads),
        grid=grid,
        in_specs=[rows((leaf, width)), rows((leaf, width))],
        out_specs=[whole(state_shape), whole((n_leaf - 1,) + state_shape)],
        out_shape=[sds(state_shape, F32), sds((n_leaf - 1,) + state_shape, BF16)],
        scratch_shapes=[pltpu.VMEM((depth,) + state_shape, F32)],
        cost_estimate=pl.CostEstimate(flops=2 * tok * width * hd, bytes_accessed=4 * tok * width, transcendentals=0),
        name="state",
    )(key_rows, value_rows)
    states = {}
    block_sum = total
    for axis in ("sub", "seq"):
        states[axis] = []
        for bit in range(bits_of(lax.axis_size(axis))):
            partner = swapped(block_sum, axis, bit)
            states[axis].append(partner)
            block_sum = block_sum + partner
    att, w = pl.pallas_call(
        functools.partial(near_kernel, heads, bits_of(leaf)),
        grid=grid,
        in_specs=[
            whole((tok // LANES, LANES)),
            whole((ntab, LANES)),
            rows((leaf, width)),
            rows((leaf, width)),
            rows((leaf, width)),
            whole((n_leaf - 1,) + state_shape),
        ],
        out_specs=[rows((leaf, width)), rows((leaf, LANES))],
        out_shape=[sds((tok, width), F32), sds((tok, LANES), F32)],
        scratch_shapes=[pltpu.VMEM((LANES, LANES), jnp.int32)],
        cost_estimate=pl.CostEstimate(
            flops=16 * tok * width * hd, bytes_accessed=10 * tok * width, transcendentals=0
        ),
        name="near",
    )(index, table, queries, key_rows, value_rows, parts)
    first = token_bits + 1
    for axis in ("sub", "seq"):
        last = axis == "seq"
        n = len(states[axis])
        att = pl.pallas_call(
            functools.partial(far_kernel, heads, first, axis, last),
            grid=grid,
            in_specs=([whole((1, width))] if last else [])
            + [rows((leaf, width)), rows((leaf, width)), rows((leaf, LANES))]
            + [whole(state_shape)] * n,
            out_specs=rows((leaf, width)),
            out_shape=sds((tok, width), BF16 if last else F32),
            scratch_shapes=[pltpu.VMEM((heads, hd, n * hd), BF16)],
            cost_estimate=pl.CostEstimate(
                flops=2 * n * tok * width * hd, bytes_accessed=10 * tok * width, transcendentals=0
            ),
            name="far_" + axis,
        )(*([gain] if last else []), att, queries, w, *states[axis])
        first += n
    return att


def solution(mesh):
    split = P(("groups", "seq", "sub"), None)
    return jax.shard_map(
        on_device,
        mesh=mesh,
        in_specs=(split, split, split, P(("groups", "seq", "sub")), P(), P()),
        out_specs=split,
        check_vma=False,
    )
```

```python
import functools

import jax
import jax.numpy as jnp
from jax import lax
from jax.experimental import pallas as pl
from jax.experimental.pallas import tpu as pltpu
from jax.sharding import PartitionSpec as P

EPS = 1e-06
LANES = 128
LEAF = 256
GROUPS = 4
F32 = jnp.float32
BF16 = jnp.bfloat16


def bits_of(size):
    return size.bit_length() - 1


def swapped(block, axis, apart):
    count = lax.axis_size(axis)
    route = []
    for low in range(count):
        high = low | 1 << apart
        if high != low and high < count:
            route += [(low, high), (high, low)]
    return lax.ppermute(block, axis, route)


def whole(shape):
    return pl.BlockSpec(shape, lambda *_: (0,) * len(shape))


def rows(block):
    return pl.BlockSpec(block, lambda i: (i,) + (0,) * (len(block) - 1))


def state_kernel(heads, leaf, k_hbm, v_hbm, total_ref, part_ref, k_buf, v_buf, acc_ref, sem):
    n_leaf = k_hbm.shape[0] // leaf
    depth = bits_of(n_leaf)
    hd = k_hbm.shape[1] // heads
    copies = []
    for step in range(n_leaf):
        here = pl.ds(step * leaf, leaf)
        pair = [
            pltpu.make_async_copy(hbm.at[here], buf.at[here], sem.at[j, step])
            for j, (hbm, buf) in enumerate(((k_hbm, k_buf), (v_hbm, v_buf)))
        ]
        for copy in pair:
            copy.start()
        copies.append(pair)
    for step in range(n_leaf):
        for copy in copies[step]:
            copy.wait()
        here = slice(step * leaf, (step + 1) * leaf)
        for h in range(heads):
            cols = slice(h * hd, (h + 1) * hd)
            value = lax.dot_general(
                v_buf[here, cols], k_buf[here, cols], (((0,), (0,)), ((), ())), preferred_element_type=F32
            )
            base = 0
            count = n_leaf
            for level in range(depth):
                count //= 2
                if (step >> level) % 2 == 0:
                    part_ref[base + (step >> (level + 1)), h] = value.astype(BF16)
                    acc_ref[level, h] = value
                    break
                value = value + acc_ref[level, h]
                base += count
            else:
                total_ref[h] = value


def level_lanes(size, heads):
    t = lax.broadcasted_iota(jnp.int32, (size, size), 0)
    s = lax.broadcasted_iota(jnp.int32, (size, size), 1)
    mixed = jnp.bitwise_xor(t, s)
    level = jnp.zeros_like(mixed)
    for bit in range(bits_of(size)):
        level = level + (mixed >= (1 << bit)).astype(jnp.int32)
    return jnp.where(s <= t, level * heads, LANES - heads)


def weight_kernel(heads, idx_ref, tbl_ref, w_ref, across_ref):
    ntab, levels, _ = tbl_ref.shape
    lane = lax.broadcasted_iota(jnp.int32, (levels, LANES), 1)
    own = lane // heads == lax.broadcasted_iota(jnp.int32, (levels, LANES), 0)
    row = lax.broadcasted_iota(jnp.int32, (ntab, LANES), 0)
    table = jnp.zeros((ntab, LANES), F32)
    for r in range(ntab):
        spread = jnp.take_along_axis(tbl_ref[r], lane % heads, axis=1)
        flat = jnp.sum(jnp.where(own, spread, 0.0), axis=0, keepdims=True)
        table = jnp.where(row == r, flat, table)
    hi = table.astype(BF16)
    rest = table - hi.astype(F32)
    mid = rest.astype(BF16)
    low = (rest - mid.astype(F32)).astype(BF16)
    pieces = jnp.concatenate([hi, mid, low], axis=0)
    for row in range(idx_ref.shape[0]):
        index = idx_ref[row : row + 1, :]
        hit = lax.broadcasted_iota(jnp.int32, (ntab, LANES), 0) == index
        hot = jnp.where(hit, 1.0, 0.0).astype(BF16)
        hot = jnp.concatenate([hot, hot, hot], axis=0)
        w = lax.dot_general(hot, pieces, (((0,), (0,)), ((), ())), preferred_element_type=F32)
        w_ref[row * LANES : (row + 1) * LANES, :] = w
        across_ref[:, row * LANES : (row + 1) * LANES] = lax.dot_general(
            pieces, hot, (((0,), (0,)), ((), ())), preferred_element_type=F32
        )


def near_kernel(heads, own, leaf, w_ref, q_ref, k_ref, v_ref, st_ref, out_ref, lane_ref):
    hd = st_ref.shape[-1]
    n_leaf = q_ref.shape[0] // leaf
    parts = leaf // LANES
    lane_ref[...] = level_lanes(LANES, heads)

    def score(step):
        found = []
        for h in own:
            cols = slice(h * hd, (h + 1) * hd)
            for part in range(parts):
                start = step * leaf
                q = q_ref[start + part * LANES : start + (part + 1) * LANES, cols]
                k = k_ref[start : start + (part + 1) * LANES, cols]
                found.append(lax.dot_general(q, k, (((1,), (1,)), ((), ())), preferred_element_type=F32))
        return found

    def finish(step, found):
        found = iter(found)
        start = step * leaf
        for i, h in enumerate(own):
            cols = slice(h * hd, (h + 1) * hd)
            mine = slice(i * hd, (i + 1) * hd)
            for part in range(parts):
                here = slice(start + part * LANES, start + (part + 1) * LANES)
                scores = next(found)
                w = w_ref[here, :]
                picked = []
                for other in range(part):
                    gap = bits_of(LANES) + (part ^ other).bit_length()
                    lane = gap * heads + h
                    block = scores[:, other * LANES : (other + 1) * LANES]
                    picked.append((w[:, lane : lane + 1] * block).astype(BF16))
                diag = jnp.take_along_axis(w, lane_ref[...] + h, axis=1)
                picked.append((diag * scores[:, part * LANES :]).astype(BF16))
                weighted = picked[0] if len(picked) == 1 else jnp.concatenate(picked, axis=1)
                v = v_ref[start : start + (part + 1) * LANES, cols]
                total = jnp.dot(weighted, v, preferred_element_type=F32)
                base = 0
                count = n_leaf
                for level in range(bits_of(n_leaf)):
                    count = count // 2
                    if (step >> level) % 2:
                        lane = (bits_of(leaf) + 1 + level) * heads + h
                        state = st_ref[base + (step >> (level + 1)), h]
                        term = lax.dot_general(
                            q_ref[here, cols], state, (((1,), (1,)), ((), ())), preferred_element_type=F32
                        )
                        total = total + w[:, lane : lane + 1] * term
                    base += count
                out_ref[mine, here] = total.T

    found = score(0)
    for step in range(n_leaf):
        ahead = score(step + 1) if step + 1 < n_leaf else None
        finish(step, found)
        found = ahead


def far_terms(heads, head, first_level, total, q, across_ref, here, stack):
    hd = q.shape[1]
    term = lax.dot_general(stack, q, (((1,), (1,)), ((), ())), preferred_element_type=F32)
    for j in range(stack.shape[0] // hd):
        lane = (first_level + j) * heads + head
        total = total + across_ref[lane : lane + 1, here] * term[j * hd : (j + 1) * hd]
    return total


def upper_of(axis, bit):
    return ((lax.axis_index(axis) >> bit) % 2).astype(F32)


def stack_states(heads, places, state_refs, stack_ref):
    hd = state_refs[0].shape[-1]
    for j, ((axis, bit), state_ref) in enumerate(zip(places, state_refs)):
        upper = upper_of(axis, bit)
        for h in range(heads):
            stack_ref[h, j * hd : (j + 1) * hd, :] = (state_ref[h] * upper).astype(BF16)


def mid_kernel(heads, first_level, places, at_once, *refs):
    n = len(places)
    att_refs, (q_ref, across_ref), state_refs = refs[:GROUPS], refs[GROUPS : GROUPS + 2], refs[GROUPS + 2 : GROUPS + 2 + n]
    out_refs, stack_ref = refs[GROUPS + 2 + n : -1], refs[-1]
    hd = state_refs[0].shape[-1]
    stack_states(heads, places, state_refs, stack_ref)
    for i in range(q_ref.shape[0] // at_once):
        here = slice(i * at_once, (i + 1) * at_once)
        for h in range(heads):
            cols = slice(h * hd, (h + 1) * hd)
            mine = slice(h // GROUPS * hd, (h // GROUPS + 1) * hd)
            total = att_refs[h % GROUPS][mine, here]
            out_refs[h % GROUPS][mine, here] = far_terms(
                heads, h, first_level, total, q_ref[here, cols], across_ref, here, stack_ref[h]
            )


def last_kernel(heads, level, place, at_once, *refs):
    gain_ref, att_refs, (q_ref, across_ref, state_ref), (out_hbm, stack_ref, out_buf, sem) = (
        refs[0], refs[1 : 1 + GROUPS], refs[1 + GROUPS : 4 + GROUPS], refs[4 + GROUPS :]
    )
    hd = state_ref.shape[-1]
    stack_states(heads, [place], [state_ref], stack_ref)
    copies = []
    for i in range(q_ref.shape[0] // at_once):
        here = slice(i * at_once, (i + 1) * at_once)
        for h in range(heads):
            cols = slice(h * hd, (h + 1) * hd)
            mine = slice(h // GROUPS * hd, (h // GROUPS + 1) * hd)
            total = att_refs[h % GROUPS][mine, here]
            total = far_terms(heads, h, level, total, q_ref[here, cols], across_ref, here, stack_ref[h])
            mean = jnp.mean(total * total, axis=0, keepdims=True)
            total = (total * lax.rsqrt(mean + EPS)).T * gain_ref[:, cols]
            out_buf[here, cols] = total.astype(BF16)
        span = pl.ds(i * at_once, at_once)
        copies.append(pltpu.make_async_copy(out_buf.at[span], out_hbm.at[span], sem.at[i]))
        copies[-1].start()
    for copy in copies:
        copy.wait()


MIB = 1 << 20
VMEM = pl.BlockSpec(memory_space=pltpu.VMEM)
HBM = pl.BlockSpec(memory_space=pltpu.HBM)


def on_device(queries, key_rows, value_rows, level_index, level_table, out_gain):
    tok, width = queries.shape
    ntab, levels, heads = level_table.shape
    hd = width // heads
    leaf = min(LEAF, tok)
    n_leaf = tok // leaf
    depth = bits_of(n_leaf)
    token_bits = bits_of(tok)
    table = jnp.pad(level_table, ((0, 0), (0, -levels % 8), (0, LANES - heads)))
    index = level_index.reshape(tok // LANES, LANES)
    gain = out_gain.reshape(1, width)
    state_shape = (heads, hd, hd)
    sds = jax.ShapeDtypeStruct
    params = lambda mib: pltpu.CompilerParams(vmem_limit_bytes=mib * MIB)
    total, parts = pl.pallas_call(
        functools.partial(state_kernel, heads, leaf),
        in_specs=[HBM, HBM],
        out_specs=[VMEM] * 2,
        out_shape=[sds(state_shape, F32), sds((n_leaf - 1,) + state_shape, BF16)],
        scratch_shapes=[
            pltpu.VMEM((tok, width), BF16),
            pltpu.VMEM((tok, width), BF16),
            pltpu.VMEM((depth,) + state_shape, F32),
            pltpu.SemaphoreType.DMA((2, n_leaf)),
        ],
        compiler_params=params(52),
        cost_estimate=pl.CostEstimate(flops=2 * tok * width * hd, bytes_accessed=4 * tok * width, transcendentals=0),
        name="state",
    )(key_rows, value_rows)
    w, across = pl.pallas_call(
        functools.partial(weight_kernel, heads),
        in_specs=[VMEM, VMEM],
        out_specs=[VMEM] * 2,
        out_shape=[sds((tok, LANES), F32), sds((LANES, tok), F32)],
        compiler_params=params(8),
        cost_estimate=pl.CostEstimate(flops=tok * LANES * 64, bytes_accessed=4 * tok * LANES, transcendentals=0),
        name="weights",
    )(index, table)
    split = [list(range(heads))[g::GROUPS] for g in range(GROUPS)]
    near = []
    for own in split:
        near.append(pl.pallas_call(
            functools.partial(near_kernel, heads, own, leaf),
            in_specs=[VMEM] * 5,
            out_specs=VMEM,
            out_shape=sds((len(own) * hd, tok), F32),
            scratch_shapes=[pltpu.VMEM((LANES, LANES), jnp.int32)],
            compiler_params=params(12),
            cost_estimate=pl.CostEstimate(
                flops=4 * len(own) * tok * width * hd, bytes_accessed=5 * tok * width, transcendentals=0
            ),
            name="near_%d" % own[0],
        )(w, queries, key_rows, value_rows, parts))
    places = [(axis, bit) for axis in ("sub", "seq") for bit in range(bits_of(lax.axis_size(axis)))]
    states = []
    block_sum = total
    for j, (axis, bit) in enumerate(places):
        partner = swapped(block_sum, axis, bit)
        if j == 0:
            partner, near[0] = lax.optimization_barrier((partner, near[0]))
        elif j == 1:
            partner, *near[1:] = lax.optimization_barrier((partner, *near[1:]))
        states.append(partner)
        block_sum = block_sum + partner
    first = token_bits + 1
    n = len(places)
    near = pl.pallas_call(
        functools.partial(mid_kernel, heads, first, places[:-1], leaf),
        in_specs=[VMEM] * (GROUPS + 2 + n - 1),
        out_specs=[VMEM] * GROUPS,
        out_shape=[sds((len(own) * hd, tok), F32) for own in split],
        input_output_aliases={g: g for g in range(GROUPS)},
        scratch_shapes=[pltpu.VMEM((heads, (n - 1) * hd, hd), BF16)],
        compiler_params=params(32),
        cost_estimate=pl.CostEstimate(
            flops=2 * n * tok * width * hd, bytes_accessed=10 * tok * width, transcendentals=0
        ),
        name="mid",
    )(*near, queries, across, *states[:-1])
    *near, states[-1] = lax.optimization_barrier((*near, states[-1]))
    return pl.pallas_call(
        functools.partial(last_kernel, heads, first + n - 1, places[-1], leaf),
        in_specs=[VMEM] * (GROUPS + 4),
        out_specs=HBM,
        out_shape=sds((tok, width), BF16),
        scratch_shapes=[
            pltpu.VMEM((heads, hd, hd), BF16),
            pltpu.VMEM((tok, width), BF16),
            pltpu.SemaphoreType.DMA((n_leaf,)),
        ],
        compiler_params=params(12),
        cost_estimate=pl.CostEstimate(
            flops=2 * tok * width * hd, bytes_accessed=10 * tok * width, transcendentals=0
        ),
        name="last",
    )(gain, *near, queries, across, states[-1])


def solution(mesh):
    split = P(("groups", "seq", "sub"), None)
    return jax.shard_map(
        on_device,
        mesh=mesh,
        in_specs=(split, split, split, P(("groups", "seq", "sub")), P(), P()),
        out_specs=split,
        check_vma=False,
    )
```
